512 devices in a mesh: dp: 8 (over z_lo), ctx: 64 (over x, z_hi, y, core).
Axes of the slice: x: 4, y: 4, z: 16 (z_hi: 2, z_lo: 8; z = z_hi * 8 + z_lo), core: 2. Of those that a mesh axis runs over, the one named last changes fastest.
Arguments:
- pre_gate: bfloat16 [2048, 16384], P('dp', 'ctx'), may hold values from -6 to 6
- values: bfloat16 [2048, 16384], P('dp', 'ctx'), may hold values from -6 to 6
- post_gate: bfloat16 [2048, 16384], P('dp', 'ctx'), may hold values from -6 to 6
- filters: float32 [256, 16384], P('ctx', 'dp'), may hold values from -0.046875 to 0.046875
- cotangent: bfloat16 [2048, 16384], P('dp', 'ctx'), may hold values from -6 to 6
Outputs:
- mixed: bfloat16 [2048, 16384], P('dp', 'ctx')
- pre_grad: bfloat16 [2048, 16384], P('dp', 'ctx')
- value_grad: bfloat16 [2048, 16384], P('dp', 'ctx')
- post_grad: bfloat16 [2048, 16384], P('dp', 'ctx')
- filter_grad: float32 [256, 16384], P('ctx', 'dp')
The draws below stay inside these ranges and needn't reach their ends.
All inputs are finite; a program needn't handle non-finite values.
Results may differ from the reference program's by a relative error of at most 0.014.
Values may be sent and summed in bfloat16 or wider, within the bound.
A program may use at most 64 MiB of HBM per device.

```python
import jax
import jax.numpy as jnp
from jax import lax

D = 2048
FG = 256
L = 16384


def levels(stream_key, shape, split, smallest, top_value):
    gain, own = 1.0, jax.random.fold_in(stream_key, 6)
    for axis_at, parts in split:
        draws = jnp.exp(jax.random.uniform(jax.random.fold_in(own, axis_at), (parts,), jnp.float32, smallest / len(split), top_value / len(split)))
        gain = gain * jnp.repeat(draws, shape[axis_at] // parts).reshape([-1 if axis == axis_at else 1 for axis in range(len(shape))])
    return gain


def gaussian(key, extent, spread, most, pieces=(), kind=jnp.bfloat16):
    result = jax.random.normal(key, extent, jnp.float32) * spread
    if len(pieces) > 0:
        result = levels(key, extent, pieces, -0.22, 0.18) * result
    return jnp.clip(result, min=-most, max=most).astype(kind)


def setup_inputs(seed: int = 0) -> dict:
    key_of = jax.random.split(jax.random.key(seed), 6)
    pre_gate = gaussian(key_of[0], (D, L), 1.0, 6.0, ((0, 8), (1, 64)))
    values = gaussian(key_of[1], (D, L), 1.0, 6.0, ((0, 8), (1, 64)))
    post_gate = gaussian(key_of[2], (D, L), 1.0, 6.0, ((0, 8), (1, 64)))
    filters = gaussian(key_of[3], (FG, L), L ** -0.5, 0.046875, ((0, 64), (1, 8)), jnp.float32)
    cotangent = gaussian(key_of[4], (D, L), 1.0, 6.0, ((0, 8), (1, 64)))
    return dict(pre_gate=pre_gate, values=values, post_gate=post_gate, filters=filters, cotangent=cotangent)


def reference(pre_gate, values, post_gate, filters, cotangent):
    count = filters.shape[0]
    length = filters.shape[1]
    points = 2 * length
    repeats = pre_gate.shape[0] // count
    filter_spec = jnp.fft.rfft(filters, n=points, axis=-1)

    def split_rows(array):
        return array.reshape(repeats, count, length)

    def one_group(carry, items):
        pre_row, value_row, post_row, cot_row = items
        gated = (pre_row.astype(jnp.float32) * value_row.astype(jnp.float32)).astype(jnp.bfloat16)
        gated_spec = jnp.fft.rfft(gated.astype(jnp.float32), n=points, axis=-1)
        conv = jnp.fft.irfft(gated_spec * filter_spec, n=points, axis=-1)[:, :length].astype(jnp.bfloat16)
        mixed = (post_row.astype(jnp.float32) * conv.astype(jnp.float32)).astype(jnp.bfloat16)
        post_grad = (cot_row.astype(jnp.float32) * conv.astype(jnp.float32)).astype(jnp.bfloat16)
        conv_grad = (cot_row.astype(jnp.float32) * post_row.astype(jnp.float32)).astype(jnp.bfloat16)
        grad_spec = jnp.fft.rfft(conv_grad.astype(jnp.float32), n=points, axis=-1)
        gated_grad = jnp.fft.irfft(jnp.conj(filter_spec) * grad_spec, n=points, axis=-1)[:, :length].astype(jnp.bfloat16)
        pre_grad = (gated_grad.astype(jnp.float32) * value_row.astype(jnp.float32)).astype(jnp.bfloat16)
        value_grad = (gated_grad.astype(jnp.float32) * pre_row.astype(jnp.float32)).astype(jnp.bfloat16)
        filter_term = jnp.fft.irfft(jnp.conj(gated_spec) * grad_spec, n=points, axis=-1)[:, :length]
        return carry + filter_term, (mixed, pre_grad, value_grad, post_grad)

    start = jnp.zeros(filters.shape, jnp.float32)
    total, outputs = lax.scan(one_group, start, (split_rows(pre_gate), split_rows(values), split_rows(post_gate), split_rows(cotangent)))
    shape = pre_gate.shape
    return outputs[0].reshape(shape), outputs[1].reshape(shape), outputs[2].reshape(shape), outputs[3].reshape(shape), total
```

```python
import functools

import jax
import jax.numpy as jnp
import numpy as np
from jax import lax
from jax.experimental import pallas as pl
from jax.experimental.pallas import tpu as pltpu
from jax.sharding import PartitionSpec as P

MESH = pl.DeviceIdType.MESH
BF = jnp.bfloat16
F32 = jnp.float32
ROWS = 8
TOKENS = 256


def tables(nb, groups):
    total = 2 * nb * TOKENS
    k1 = np.arange(nb)[:, None] + 0.5
    angle = 2 * np.pi * k1 * np.arange(nb)[None, :] / (2 * nb)
    first = np.concatenate([np.cos(angle), -np.sin(angle)], axis=0)
    own = nb // groups
    spread = np.repeat(first, ROWS, axis=1)
    column = np.arange(nb * ROWS)
    within = column % (nb * 4)
    block = (within // (own * 4)) * own + (within % (own * 4)) // 4
    filter_spread = first[:, block]
    row = np.arange(nb * 4)
    block_out = (row // (own * 4)) * own + (row % (own * 4)) // 4
    filter_back = first[:, block_out].T
    t = np.arange(TOKENS)
    twist = 2 * np.pi * k1 * t[None, :] / total
    turn = np.stack([np.cos(twist), np.sin(twist)])
    inner = 2 * np.pi * ((t[:, None] * t[None, :]) % TOKENS) / TOKENS
    c, s = np.cos(inner), np.sin(inner)
    third = np.block([[c, -s], [s, c]])
    to = lambda a: np.asarray(a, np.float32).astype(jnp.bfloat16)
    return (
        to(spread),
        to(spread.T),
        to(filter_spread),
        to(filter_back),
        to(third),
        to(third.T),
        np.asarray(turn, np.float32),
    )


def dot(a, b):
    return lax.dot_general(a, b, (((1,), (0,)), ((), ())), preferred_element_type=F32)


def main_kernel(
    nb, groups,
    pre_h, val_h, post_h, cot_h, filt_h, e_h, et_h, ef_h, eft_h, t3_h, t3i_h, tw_h,
    out_h, fgr_h,
    pre, val, post, cot, filt, e, et, ef, eft, t3, t3i, tw,
    xs, recv, fb, w, wt, wf, wtf, a, b, spec, fspec, prod, u, y, sx, rx, fgs,
    in_sem, send_sem, recv_sem,
):
    own = nb // groups
    chunk = own * 4
    half = nb * 4
    dp = lax.axis_index("dp")
    ctx = lax.axis_index("ctx")
    core = lax.rem(ctx, 2)
    chip = lax.div(ctx, 2)
    far = lax.rem(dp + groups // 2, groups)
    partner = ctx + 1 - 2 * core

    pairs = (
        (pre_h, pre), (val_h, val), (post_h, post), (cot_h, cot), (filt_h, filt), (tw_h, tw),
        (e_h, e), (et_h, et), (ef_h, ef), (eft_h, eft), (t3_h, t3), (t3i_h, t3i),
    )
    loads = [pltpu.make_async_copy(s, d, in_sem.at[i]) for i, (s, d) in enumerate(pairs)]
    for load in loads:
        load.start()

    barrier = pltpu.get_barrier_semaphore()

    def greet(j, carry):
        pl.semaphore_signal(barrier, inc=1, device_id={"dp": far, "ctx": j}, device_id_type=MESH)
        return carry

    lax.fori_loop(0, nb, greet, 0)
    pl.semaphore_signal(barrier, inc=1, device_id={"dp": dp, "ctx": partner}, device_id_type=MESH)
    for i in range(1, groups):
        pl.semaphore_signal(
            barrier, inc=1, device_id={"dp": lax.rem(dp + i, groups), "ctx": ctx}, device_id_type=MESH
        )

    for load in loads[:5]:
        load.wait()
    xs[0] = (pre[...].astype(F32) * val[...].astype(F32)).astype(BF)
    xs[1] = (cot[...].astype(F32) * post[...].astype(F32)).astype(BF)
    mine = pl.multiple_of(core * half + dp * chunk, chunk)
    fb[pl.ds(mine, chunk), :] = jnp.concatenate(
        [filt[:, i * TOKENS : (i + 1) * TOKENS] for i in range(own)], axis=0
    ).astype(BF)

    pl.semaphore_wait(barrier, nb + groups)

    for i in range(1, groups):
        pltpu.make_async_remote_copy(
            src_ref=fb.at[pl.ds(mine, chunk), :],
            dst_ref=fb.at[pl.ds(mine, chunk), :],
            send_sem=send_sem.at[0],
            recv_sem=recv_sem.at[0],
            device_id={"dp": lax.rem(dp + i, groups), "ctx": ctx},
            device_id_type=MESH,
        ).start()

    place = pl.multiple_of(ctx * ROWS, ROWS)

    def send_in(m, carry):
        rows = pl.ds(pl.multiple_of(m * ROWS, ROWS), ROWS)
        for signal in range(2):
            pltpu.make_async_remote_copy(
                src_ref=xs.at[signal, rows, :],
                dst_ref=recv.at[pl.ds(place, ROWS), :],
                send_sem=send_sem.at[1],
                recv_sem=recv_sem.at[1],
                device_id={"dp": far, "ctx": 2 * m + signal},
                device_id_type=MESH,
            ).start()
        return carry

    lax.fori_loop(0, nb // 2, send_in, 0)

    for load in loads[5:]:
        load.wait()
    wide = 2 * nb

    def spread_rows(s, carry):
        rows = pl.ds(pl.multiple_of(s * wide, wide), wide)
        column = lax.broadcasted_iota(jnp.int32, (wide, nb * ROWS), 1)
        keep = ((column & (ROWS - 1)) == s).astype(F32)
        w[rows, :] = (e[...].astype(F32) * keep).astype(BF)
        group = jnp.where(column >= half, 4, 0) + (column & 3)
        keep = (group == s).astype(F32)
        wf[rows, :] = (ef[...].astype(F32) * keep).astype(BF)
        return carry

    lax.fori_loop(0, ROWS, spread_rows, 0)
    row = lax.broadcasted_iota(jnp.int32, (nb * ROWS, wide), 0)
    for s in range(ROWS):
        keep = ((row & (ROWS - 1)) == s).astype(F32)
        wt[:, s * wide : (s + 1) * wide] = (et[...].astype(F32) * keep).astype(BF)
    row = lax.broadcasted_iota(jnp.int32, (half, wide), 0)
    for s in range(4):
        keep = ((row & 3) == s).astype(F32)
        wtf[:, s * wide : (s + 1) * wide] = (eft[...].astype(F32) * keep).astype(BF)

    def wait_bytes(ref, sem):
        pltpu.make_async_copy(ref, ref, sem).wait()

    def forward(source, table, result):
        a[...] = dot(table[...], source[...])

        def one(s, carry):
            ar = a[pl.ds(pl.multiple_of(s * wide, wide), nb), :]
            ai = a[pl.ds(pl.multiple_of(s * wide + nb, nb), nb), :]
            tc, ts = tw[0], tw[1]
            rows = pl.ds(pl.multiple_of(s * nb, nb), nb)
            b[rows, 0:TOKENS] = (ar * tc + ai * ts).astype(BF)
            b[rows, TOKENS:] = (ai * tc - ar * ts).astype(BF)
            return carry

        lax.fori_loop(0, ROWS, one, 0)
        result[...] = dot(b[...], t3[...])

    def backward(count):
        spec_rows = count * nb
        v = dot(prod[0:spec_rows, :], t3i[...])
        scale = 2.0 / (2 * nb * TOKENS)
        tc, ts = tw[0] * scale, tw[1] * scale
        for s in range(count):
            vr = v[s * nb : (s + 1) * nb, 0:TOKENS]
            vi = v[s * nb : (s + 1) * nb, TOKENS:]
            u[s * wide : s * wide + nb, :] = (vr * tc - vi * ts).astype(BF)
            u[s * wide + nb : (s + 1) * wide, :] = (vr * ts + vi * tc).astype(BF)

    wait_bytes(fb.at[pl.ds(0, (groups - 1) * chunk), :], recv_sem.at[0])
    side = pl.ds(pl.multiple_of(core * half, half), half)
    swap = pltpu.make_async_remote_copy(
        src_ref=fb.at[side, :],
        dst_ref=fb.at[side, :],
        send_sem=send_sem.at[2],
        recv_sem=recv_sem.at[2],
        device_id={"dp": dp, "ctx": partner},
        device_id_type=MESH,
    )
    swap.start()
    swap.wait()
    forward(fb, wf, fspec)

    wait_bytes(recv, recv_sem.at[1])
    forward(recv, w, spec)

    sign = (1 - 2 * core).astype(F32)
    theirs = pl.ds(pl.multiple_of((1 - core) * half, half), half)
    sx[...] = spec[theirs, :].astype(BF)
    fr, fi = fspec[:, 0:TOKENS], fspec[:, TOKENS:] * sign
    xr, xi = spec[:, 0:TOKENS], spec[:, TOKENS:]
    prod[:, 0:TOKENS] = (fr * xr - fi * xi).astype(BF)
    prod[:, TOKENS:] = (fr * xi + fi * xr).astype(BF)
    cross = pltpu.make_async_remote_copy(
        src_ref=sx,
        dst_ref=rx,
        send_sem=send_sem.at[3],
        recv_sem=recv_sem.at[3],
        device_id={"dp": dp, "ctx": partner},
        device_id_type=MESH,
    )
    cross.start()
    backward(ROWS)
    y[...] = dot(wt[...], u[...]).astype(BF)

    home = pl.ds(pl.multiple_of(chip * ROWS, ROWS), ROWS)

    def send_out(j, carry):
        pltpu.make_async_remote_copy(
            src_ref=y.at[pl.ds(pl.multiple_of(j * ROWS, ROWS), ROWS), :],
            dst_ref=out_h.at[core, home, :],
            send_sem=send_sem.at[4],
            recv_sem=recv_sem.at[4],
            device_id={"dp": far, "ctx": j},
            device_id_type=MESH,
        ).start()
        return carry

    lax.fori_loop(0, nb, send_out, 0)

    cross.wait()
    ours = pl.ds(pl.multiple_of(core * half, half), half)
    xr, xi = spec[ours, 0:TOKENS], spec[ours, TOKENS:]
    gr, gi = rx[:, 0:TOKENS].astype(F32), rx[:, TOKENS:].astype(F32)
    prod[0:half, 0:TOKENS] = (xr * gr + xi * gi).astype(BF)
    prod[0:half, TOKENS:] = ((xr * gi - xi * gr) * sign).astype(BF)
    backward(4)
    fgs[...] = dot(wtf[...], u[0 : 4 * wide, :]).astype(BF)
    here = pl.multiple_of(dp * chunk, chunk)
    keep_own = pltpu.make_async_copy(
        fgs.at[pl.ds(here, chunk), :], fgr_h.at[pl.ds(here, chunk), :], in_sem.at[0]
    )
    keep_own.start()
    for i in range(1, groups):
        peer = lax.rem(dp + i, groups)
        pltpu.make_async_remote_copy(
            src_ref=fgs.at[pl.ds(pl.multiple_of(peer * chunk, chunk), chunk), :],
            dst_ref=fgr_h.at[pl.ds(here, chunk), :],
            send_sem=send_sem.at[5],
            recv_sem=recv_sem.at[5],
            device_id={"dp": peer, "ctx": ctx},
            device_id_type=MESH,
        ).start()

    keep_own.wait()
    others = fb.at[pl.ds(0, (groups - 1) * chunk), :]
    wait_bytes(others, send_sem.at[0])
    wait_bytes(recv, send_sem.at[1])
    wait_bytes(y, send_sem.at[4])
    wait_bytes(others, send_sem.at[5])
    wait_bytes(others, recv_sem.at[5])
    wait_bytes(y, recv_sem.at[4])


def last_kernel(own, groups, pre, val, post, cot, back, fgr, mixed, pre_grad, value_grad, post_grad, filter_grad):
    conv = back[0].astype(F32)
    mixed[...] = (post[...].astype(F32) * conv).astype(BF)
    post_grad[...] = (cot[...].astype(F32) * conv).astype(BF)
    grad = back[1].astype(F32)
    pre_grad[...] = (grad * val[...].astype(F32)).astype(BF)
    value_grad[...] = (grad * pre[...].astype(F32)).astype(BF)
    chunk = own * 4
    total = fgr[0:chunk, :].astype(F32)
    for i in range(1, groups):
        total = total + fgr[i * chunk : (i + 1) * chunk, :].astype(F32)
    for i in range(own):
        filter_grad[:, i * TOKENS : (i + 1) * TOKENS] = total[4 * i : 4 * i + 4, :]


def body(pre_gate, values, post_gate, filters, cotangent):
    nb = lax.axis_size("ctx")
    groups = lax.axis_size("dp")
    own = nb // groups
    rows = nb * 4
    consts = tables(nb, groups)
    anywhere = pl.BlockSpec(memory_space=pl.ANY)
    vmem = pl.BlockSpec(memory_space=pltpu.VMEM)
    sig = (rows, TOKENS)
    scratch = [
        pltpu.VMEM(sig, BF), pltpu.VMEM(sig, BF), pltpu.VMEM(sig, BF), pltpu.VMEM(sig, BF),
        pltpu.VMEM(filters.shape, F32),
        *[pltpu.VMEM(c.shape, BF) for c in consts[:6]],
        pltpu.VMEM(consts[6].shape, F32),
        pltpu.VMEM((2,) + sig, BF),
        pltpu.VMEM((nb * ROWS, TOKENS), BF),
        pltpu.VMEM((nb * ROWS, TOKENS), BF),
        pltpu.VMEM((ROWS * 2 * nb, nb * ROWS), BF),
        pltpu.VMEM((nb * ROWS, ROWS * 2 * nb), BF),
        pltpu.VMEM((ROWS * 2 * nb, nb * ROWS), BF),
        pltpu.VMEM((nb * 4, 4 * 2 * nb), BF),
        pltpu.VMEM((ROWS * 2 * nb, TOKENS), F32),
        pltpu.VMEM((ROWS * nb, 2 * TOKENS), BF),
        pltpu.VMEM((ROWS * nb, 2 * TOKENS), F32),
        pltpu.VMEM((ROWS * nb, 2 * TOKENS), F32),
        pltpu.VMEM((ROWS * nb, 2 * TOKENS), BF),
        pltpu.VMEM((ROWS * 2 * nb, TOKENS), BF),
        pltpu.VMEM((nb * ROWS, TOKENS), BF),
        pltpu.VMEM((4 * nb, 2 * TOKENS), BF),
        pltpu.VMEM((4 * nb, 2 * TOKENS), BF),
        pltpu.VMEM((nb * 4, TOKENS), BF),
        pltpu.SemaphoreType.DMA((12,)),
        pltpu.SemaphoreType.DMA((6,)),
        pltpu.SemaphoreType.DMA((6,)),
    ]
    back, fgr = pl.pallas_call(
        functools.partial(main_kernel, nb, groups),
        out_shape=(jax.ShapeDtypeStruct((2,) + sig, BF), jax.ShapeDtypeStruct(sig, BF)),
        in_specs=[anywhere] * 12,
        out_specs=(anywhere, anywhere),
        scratch_shapes=scratch,
        compiler_params=pltpu.CompilerParams(collective_id=0, has_side_effects=True),
        name="long_conv",
    )(pre_gate, values, post_gate, cotangent, filters, *consts)
    shape = jax.ShapeDtypeStruct(pre_gate.shape, BF)
    mixed, pre_grad, value_grad, post_grad, filter_grad = pl.pallas_call(
        functools.partial(last_kernel, own, groups),
        out_shape=(shape, shape, shape, shape, jax.ShapeDtypeStruct(filters.shape, F32)),
        in_specs=[vmem] * 6,
        out_specs=(vmem,) * 5,
        name="gates",
    )(pre_gate, values, post_gate, cotangent, back, fgr)
    return (mixed, pre_grad, value_grad, post_grad, filter_grad)


def solution(mesh):
    big = P("dp", "ctx")
    return jax.shard_map(
        body,
        mesh=mesh,
        in_specs=(big, big, big, P("ctx", "dp"), big),
        out_specs=(big, big, big, big, P("ctx", "dp")),
        check_vma=False,
    )
```

```python
import functools

import jax
import jax.numpy as jnp
import numpy as np
from jax import lax
from jax.experimental import pallas as pl
from jax.experimental.pallas import tpu as pltpu
from jax.sharding import PartitionSpec as P

MESH = pl.DeviceIdType.MESH
BF = jnp.bfloat16
F32 = jnp.float32
ROWS = 8
TOKENS = 256


def tables(nb, groups):
    total = 2 * nb * TOKENS
    k1 = np.arange(nb)[:, None] + 0.5
    angle = 2 * np.pi * k1 * np.arange(nb)[None, :] / (2 * nb)
    first = np.concatenate([np.cos(angle), -np.sin(angle)], axis=0)
    own = nb // groups
    spread = np.repeat(first, ROWS, axis=1)
    row = np.arange(nb * 4)
    place, inside = row // (own * 4), row % (own * 4)
    lags = 2 * (place % (groups // 2)) + place // (groups // 2)
    block = lags * own + inside // 4
    filter_spread = np.tile(first[:, block], (1, 2))
    filter_back = first[:, block].T
    t = np.arange(TOKENS)
    twist = 2 * np.pi * k1 * t[None, :] / total
    turn = np.stack([np.cos(twist), np.sin(twist)])
    inner = 2 * np.pi * ((t[:, None] * t[None, :]) % TOKENS) / TOKENS
    c, s = np.cos(inner), np.sin(inner)
    third = np.block([[c, -s], [s, c]])
    to = lambda a: np.asarray(a, np.float32).astype(jnp.bfloat16)
    return (
        to(spread),
        to(spread.T),
        to(filter_spread),
        to(filter_back),
        to(third),
        to(third.T),
        np.asarray(turn, np.float32),
    )


def dot(a, b):
    return lax.dot_general(a, b, (((1,), (0,)), ((), ())), preferred_element_type=F32)


def main_kernel(
    nb, groups,
    pre_h, val_h, post_h, cot_h, filt_h, e_h, et_h, ef_h, eft_h, t3_h, t3i_h, tw_h,
    out_h, fgr_h,
    pre, val, post, cot, filt, e, et, ef, eft, t3, t3i, tw,
    xs, recv, fb, w, wt, wf, wtf, a, b, spec, fspec, prod, u, y, sx, rx, fgs, fgf, fgn, fgt,
    in_sem, send_sem, recv_sem,
):
    own = nb // groups
    chunk = own * 4
    half = nb * 4
    dp = lax.axis_index("dp")
    ctx = lax.axis_index("ctx")
    core = lax.rem(ctx, 2)
    chip = lax.div(ctx, 2)
    far = lax.rem(dp + groups // 2, groups)
    partner = ctx + 1 - 2 * core
    parity = lax.rem(dp, 2)
    near = dp + 1 - 2 * parity
    rank = lax.div(dp, 2)
    quarter = half // 2

    pairs = (
        (pre_h, pre), (val_h, val), (post_h, post), (cot_h, cot), (filt_h, filt), (tw_h, tw),
        (e_h, e), (et_h, et), (ef_h, ef), (eft_h, eft), (t3_h, t3), (t3i_h, t3i),
    )
    loads = [pltpu.make_async_copy(s, d, in_sem.at[i]) for i, (s, d) in enumerate(pairs)]
    for load in loads:
        load.start()

    barrier = pltpu.get_barrier_semaphore()

    def greet(j, carry):
        pl.semaphore_signal(barrier, inc=1, device_id={"dp": far, "ctx": j}, device_id_type=MESH)
        return carry

    lax.fori_loop(0, nb, greet, 0)
    pl.semaphore_signal(barrier, inc=1, device_id={"dp": dp, "ctx": partner}, device_id_type=MESH)
    pl.semaphore_signal(barrier, inc=1, device_id={"dp": near, "ctx": ctx}, device_id_type=MESH)
    even = [i for i in range(2, groups, 2)]
    greeted = [i for i in even if i != groups // 2]
    for i in greeted:
        pl.semaphore_signal(
            barrier, inc=1, device_id={"dp": lax.rem(dp + i, groups), "ctx": ctx}, device_id_type=MESH
        )

    for load in loads[:5]:
        load.wait()
    xs[0] = (pre[...].astype(F32) * val[...].astype(F32)).astype(BF)
    xs[1] = (cot[...].astype(F32) * post[...].astype(F32)).astype(BF)
    mine = pl.multiple_of(core * half + parity * quarter + rank * chunk, chunk)
    fb[pl.ds(mine, chunk), :] = jnp.concatenate(
        [filt[:, i * TOKENS : (i + 1) * TOKENS] for i in range(own)], axis=0
    ).astype(BF)

    pl.semaphore_wait(barrier, nb + 2 + len(greeted))

    def wait_bytes(ref, sem):
        pltpu.make_async_copy(ref, ref, sem).wait()

    for i in even:
        pltpu.make_async_remote_copy(
            src_ref=fb.at[pl.ds(mine, chunk), :],
            dst_ref=fb.at[pl.ds(mine, chunk), :],
            send_sem=send_sem.at[0],
            recv_sem=recv_sem.at[0],
            device_id={"dp": lax.rem(dp + i, groups), "ctx": ctx},
            device_id_type=MESH,
        ).start()

    place = pl.multiple_of(ctx * ROWS, ROWS)

    def send_rows(signal):
        def one(m, carry):
            rows = pl.ds(pl.multiple_of(m * ROWS, ROWS), ROWS)
            pltpu.make_async_remote_copy(
                src_ref=xs.at[signal, rows, :],
                dst_ref=recv.at[pl.ds(place, ROWS), :],
                send_sem=send_sem.at[1],
                recv_sem=recv_sem.at[1],
                device_id={"dp": far, "ctx": 2 * m + signal},
                device_id_type=MESH,
            ).start()
            return carry

        lax.fori_loop(0, nb // 2, one, 0)

    send_rows(0)

    for load in loads[5:]:
        load.wait()
    wide = 2 * nb

    def spread_rows(s, carry):
        rows = pl.ds(pl.multiple_of(s * wide, wide), wide)
        column = lax.broadcasted_iota(jnp.int32, (wide, nb * ROWS), 1)
        keep = ((column & (ROWS - 1)) == s).astype(F32)
        w[rows, :] = (e[...].astype(F32) * keep).astype(BF)
        group = jnp.where(column >= half, 4, 0) + (column & 3)
        keep = (group == s).astype(F32)
        wf[rows, :] = (ef[...].astype(F32) * keep).astype(BF)
        return carry

    lax.fori_loop(0, ROWS, spread_rows, 0)

    if even:
        wait_bytes(fb.at[pl.ds(0, len(even) * chunk), :], recv_sem.at[0])
    known = pl.ds(pl.multiple_of(core * half + parity * quarter, quarter), quarter)
    pass_on = pltpu.make_async_remote_copy(
        src_ref=fb.at[known, :],
        dst_ref=fb.at[known, :],
        send_sem=send_sem.at[6],
        recv_sem=recv_sem.at[6],
        device_id={"dp": near, "ctx": ctx},
        device_id_type=MESH,
    )
    pass_on.start()
    wait_bytes(xs.at[0], send_sem.at[1])
    send_rows(1)

    row = lax.broadcasted_iota(jnp.int32, (nb * ROWS, wide), 0)
    for s in range(ROWS):
        keep = ((row & (ROWS - 1)) == s).astype(F32)
        wt[:, s * wide : (s + 1) * wide] = (et[...].astype(F32) * keep).astype(BF)
    row = lax.broadcasted_iota(jnp.int32, (half, wide), 0)
    for s in range(4):
        keep = ((row & 3) == s).astype(F32)
        wtf[:, s * wide : (s + 1) * wide] = (eft[...].astype(F32) * keep).astype(BF)

    def forward(source, table, result):
        a[...] = dot(table[...], source[...])

        def one(s, carry):
            ar = a[pl.ds(pl.multiple_of(s * wide, wide), nb), :]
            ai = a[pl.ds(pl.multiple_of(s * wide + nb, nb), nb), :]
            tc, ts = tw[0], tw[1]
            rows = pl.ds(pl.multiple_of(s * nb, nb), nb)
            b[rows, 0:TOKENS] = (ar * tc + ai * ts).astype(BF)
            b[rows, TOKENS:] = (ai * tc - ar * ts).astype(BF)
            return carry

        lax.fori_loop(0, ROWS, one, 0)
        result[...] = dot(b[...], t3[...])

    def backward(count):
        spec_rows = count * nb
        v = dot(prod[0:spec_rows, :], t3i[...])
        scale = 2.0 / (2 * nb * TOKENS)
        tc, ts = tw[0] * scale, tw[1] * scale
        for s in range(count):
            vr = v[s * nb : (s + 1) * nb, 0:TOKENS]
            vi = v[s * nb : (s + 1) * nb, TOKENS:]
            u[s * wide : s * wide + nb, :] = (vr * tc - vi * ts).astype(BF)
            u[s * wide + nb : (s + 1) * wide, :] = (vr * ts + vi * tc).astype(BF)

    pass_on.wait()
    side = pl.ds(pl.multiple_of(core * half, half), half)
    swap = pltpu.make_async_remote_copy(
        src_ref=fb.at[side, :],
        dst_ref=fb.at[side, :],
        send_sem=send_sem.at[2],
        recv_sem=recv_sem.at[2],
        device_id={"dp": dp, "ctx": partner},
        device_id_type=MESH,
    )
    swap.start()
    swap.wait()
    forward(fb, wf, fspec)

    wait_bytes(recv, recv_sem.at[1])
    forward(recv, w, spec)

    sign = (1 - 2 * core).astype(F32)
    theirs = pl.ds(pl.multiple_of((1 - core) * half, half), half)
    sx[...] = spec[theirs, :].astype(BF)
    fr, fi = fspec[:, 0:TOKENS], fspec[:, TOKENS:] * sign
    xr, xi = spec[:, 0:TOKENS], spec[:, TOKENS:]
    prod[:, 0:TOKENS] = (fr * xr - fi * xi).astype(BF)
    prod[:, TOKENS:] = (fr * xi + fi * xr).astype(BF)
    cross = pltpu.make_async_remote_copy(
        src_ref=sx,
        dst_ref=rx,
        send_sem=send_sem.at[3],
        recv_sem=recv_sem.at[3],
        device_id={"dp": dp, "ctx": partner},
        device_id_type=MESH,
    )
    cross.start()
    backward(ROWS)
    y[...] = dot(wt[...], u[...]).astype(BF)

    home = pl.ds(pl.multiple_of(chip * ROWS, ROWS), ROWS)

    def send_out(j, carry):
        pltpu.make_async_remote_copy(
            src_ref=y.at[pl.ds(pl.multiple_of(j * ROWS, ROWS), ROWS), :],
            dst_ref=out_h.at[core, home, :],
            send_sem=send_sem.at[4],
            recv_sem=recv_sem.at[4],
            device_id={"dp": far, "ctx": j},
            device_id_type=MESH,
        ).start()
        return carry

    lax.fori_loop(0, nb, send_out, 0)

    cross.wait()
    ours = pl.ds(pl.multiple_of(core * half, half), half)
    xr, xi = spec[ours, 0:TOKENS], spec[ours, TOKENS:]
    gr, gi = rx[:, 0:TOKENS].astype(F32), rx[:, TOKENS:].astype(F32)
    prod[0:half, 0:TOKENS] = (xr * gr + xi * gi).astype(BF)
    prod[0:half, TOKENS:] = ((xr * gi - xi * gr) * sign).astype(BF)
    backward(4)
    fg = dot(wtf[...], u[0 : 4 * wide, :])
    fgf[...] = fg
    fgs[...] = fg.astype(BF)
    hop = pltpu.make_async_remote_copy(
        src_ref=fgs.at[pl.ds(pl.multiple_of((1 - parity) * quarter, quarter), quarter), :],
        dst_ref=fgn,
        send_sem=send_sem.at[7],
        recv_sem=recv_sem.at[7],
        device_id={"dp": near, "ctx": ctx},
        device_id_type=MESH,
    )
    hop.start()
    hop.wait()
    kept = fgf[pl.ds(pl.multiple_of(parity * quarter, quarter), quarter), :]
    fgt[...] = (kept + fgn[...].astype(F32)).astype(BF)
    here = pl.multiple_of(rank * chunk, chunk)
    keep_own = pltpu.make_async_copy(
        fgt.at[pl.ds(here, chunk), :], fgr_h.at[pl.ds(here, chunk), :], in_sem.at[0]
    )
    keep_own.start()
    for i in even:
        peer = lax.rem(dp + i, groups)
        pltpu.make_async_remote_copy(
            src_ref=fgt.at[pl.ds(pl.multiple_of(lax.div(peer, 2) * chunk, chunk), chunk), :],
            dst_ref=fgr_h.at[pl.ds(here, chunk), :],
            send_sem=send_sem.at[5],
            recv_sem=recv_sem.at[5],
            device_id={"dp": peer, "ctx": ctx},
            device_id_type=MESH,
        ).start()

    keep_own.wait()
    if even:
        others = fb.at[pl.ds(0, len(even) * chunk), :]
        wait_bytes(others, send_sem.at[0])
        wait_bytes(others, send_sem.at[5])
        wait_bytes(others, recv_sem.at[5])
    wait_bytes(xs.at[1], send_sem.at[1])
    wait_bytes(y, send_sem.at[4])
    wait_bytes(y, recv_sem.at[4])


def last_kernel(own, groups, pre, val, post, cot, back, fgr, mixed, pre_grad, value_grad, post_grad, filter_grad):
    conv = back[0].astype(F32)
    mixed[...] = (post[...].astype(F32) * conv).astype(BF)
    post_grad[...] = (cot[...].astype(F32) * conv).astype(BF)
    grad = back[1].astype(F32)
    pre_grad[...] = (grad * val[...].astype(F32)).astype(BF)
    value_grad[...] = (grad * pre[...].astype(F32)).astype(BF)
    chunk = own * 4
    total = fgr[0:chunk, :].astype(F32)
    for i in range(1, groups // 2):
        total = total + fgr[i * chunk : (i + 1) * chunk, :].astype(F32)
    for i in range(own):
        filter_grad[:, i * TOKENS : (i + 1) * TOKENS] = total[4 * i : 4 * i + 4, :]


def body(pre_gate, values, post_gate, filters, cotangent):
    nb = lax.axis_size("ctx")
    groups = lax.axis_size("dp")
    own = nb // groups
    rows = nb * 4
    consts = tables(nb, groups)
    anywhere = pl.BlockSpec(memory_space=pl.ANY)
    vmem = pl.BlockSpec(memory_space=pltpu.VMEM)
    sig = (rows, TOKENS)
    scratch = [
        pltpu.VMEM(sig, BF), pltpu.VMEM(sig, BF), pltpu.VMEM(sig, BF), pltpu.VMEM(sig, BF),
        pltpu.VMEM(filters.shape, F32),
        *[pltpu.VMEM(c.shape, BF) for c in consts[:6]],
        pltpu.VMEM(consts[6].shape, F32),
        pltpu.VMEM((2,) + sig, BF),
        pltpu.VMEM((nb * ROWS, TOKENS), BF),
        pltpu.VMEM((nb * ROWS, TOKENS), BF),
        pltpu.VMEM((ROWS * 2 * nb, nb * ROWS), BF),
        pltpu.VMEM((nb * ROWS, ROWS * 2 * nb), BF),
        pltpu.VMEM((ROWS * 2 * nb, nb * ROWS), BF),
        pltpu.VMEM((nb * 4, 4 * 2 * nb), BF),
        pltpu.VMEM((ROWS * 2 * nb, TOKENS), F32),
        pltpu.VMEM((ROWS * nb, 2 * TOKENS), BF),
        pltpu.VMEM((ROWS * nb, 2 * TOKENS), F32),
        pltpu.VMEM((ROWS * nb, 2 * TOKENS), F32),
        pltpu.VMEM((ROWS * nb, 2 * TOKENS), BF),
        pltpu.VMEM((ROWS * 2 * nb, TOKENS), BF),
        pltpu.VMEM((nb * ROWS, TOKENS), BF),
        pltpu.VMEM((4 * nb, 2 * TOKENS), BF),
        pltpu.VMEM((4 * nb, 2 * TOKENS), BF),
        pltpu.VMEM((nb * 4, TOKENS), BF),
        pltpu.VMEM((nb * 4, TOKENS), F32),
        pltpu.VMEM((nb * 2, TOKENS), BF),
        pltpu.VMEM((nb * 2, TOKENS), BF),
        pltpu.SemaphoreType.DMA((12,)),
        pltpu.SemaphoreType.DMA((8,)),
        pltpu.SemaphoreType.DMA((8,)),
    ]
    back, fgr = pl.pallas_call(
        functools.partial(main_kernel, nb, groups),
        out_shape=(jax.ShapeDtypeStruct((2,) + sig, BF), jax.ShapeDtypeStruct((nb * 2, TOKENS), BF)),
        in_specs=[anywhere] * 12,
        out_specs=(anywhere, anywhere),
        scratch_shapes=scratch,
        compiler_params=pltpu.CompilerParams(collective_id=0, has_side_effects=True),
        name="long_conv",
    )(pre_gate, values, post_gate, cotangent, filters, *consts)
    shape = jax.ShapeDtypeStruct(pre_gate.shape, BF)
    mixed, pre_grad, value_grad, post_grad, filter_grad = pl.pallas_call(
        functools.partial(last_kernel, own, groups),
        out_shape=(shape, shape, shape, shape, jax.ShapeDtypeStruct(filters.shape, F32)),
        in_specs=[vmem] * 6,
        out_specs=(vmem,) * 5,
        name="gates",
    )(pre_gate, values, post_gate, cotangent, back, fgr)
    return (mixed, pre_grad, value_grad, post_grad, filter_grad)


def solution(mesh):
    big = P("dp", "ctx")
    return jax.shard_map(
        body,
        mesh=mesh,
        in_specs=(big, big, big, P("ctx", "dp"), big),
        out_specs=(big, big, big, big, P("ctx", "dp")),
        check_vma=False,
    )
```

```python
import functools

import jax
import jax.numpy as jnp
import numpy as np
from jax import lax
from jax.experimental import pallas as pl
from jax.experimental.pallas import tpu as pltpu
from jax.sharding import PartitionSpec as P

MESH = pl.DeviceIdType.MESH
BF = jnp.bfloat16
F32 = jnp.float32
ROWS = 8
TOKENS = 256


def tables(nb, groups):
    total = 2 * nb * TOKENS
    k1 = np.arange(nb)[:, None] + 0.5
    angle = 2 * np.pi * k1 * np.arange(nb)[None, :] / (2 * nb)
    first = np.concatenate([np.cos(angle), -np.sin(angle)], axis=0)
    spread = np.repeat(first, ROWS, axis=1)
    filter_spread = np.repeat(first, 4, axis=1)
    filter_back = np.repeat(first, 2, axis=1).T
    t = np.arange(TOKENS)
    twist = 2 * np.pi * k1 * t[None, :] / total
    turn = np.stack([np.cos(twist), np.sin(twist)])
    inner = 2 * np.pi * ((t[:, None] * t[None, :]) % TOKENS) / TOKENS
    c, s = np.cos(inner), np.sin(inner)
    third = np.block([[c, -s], [s, c]])
    to = lambda a: np.asarray(a, np.float32).astype(jnp.bfloat16)
    return (
        to(spread),
        to(spread.T),
        to(filter_spread),
        to(filter_back),
        to(third),
        to(third.T),
        np.asarray(turn, np.float32),
    )


def dot(a, b):
    return lax.dot_general(a, b, (((1,), (0,)), ((), ())), preferred_element_type=F32)


def main_kernel(
    nb, groups,
    pre_h, val_h, post_h, cot_h, filt_h, e_h, et_h, ef_h, eft_h, t3_h, t3i_h, tw_h,
    out_h, fgr_h,
    pre, val, post, cot, filt, e, et, ef, eft, t3, t3i, tw,
    xs, recv, fbs, fb, w, wt, wf, wtf, a, b, spec, fspec, prod, u, y, sx, rx, fgs,
    in_sem, send_sem, recv_sem, row_sem,
):
    own = nb // groups
    chunk = own * 4
    piece = own * 2
    wide = 2 * nb
    dp = lax.axis_index("dp")
    ctx = lax.axis_index("ctx")
    core = lax.rem(ctx, 2)
    chip = lax.div(ctx, 2)
    parity = lax.rem(dp, 2)
    base = dp - parity
    far = lax.rem(base + groups // 2, groups)
    rank = lax.div(dp, 2)
    partner = ctx + 1 - 2 * core
    holder = core == parity

    barrier = pltpu.get_barrier_semaphore()

    def greet(j, carry):
        for part in range(2):
            pl.semaphore_signal(barrier, inc=1, device_id={"dp": far + part, "ctx": j}, device_id_type=MESH)
        return carry

    lax.fori_loop(0, nb, greet, 0)
    line = [(dp, partner)]
    for side in range(2):
        line.append((base + 1 - parity, 2 * chip + side))
        for i in range(2, groups):
            if i // 2 != groups // 4:
                line.append((lax.rem(base + i, groups), 2 * chip + side))
    for place, seat in line:
        pl.semaphore_signal(barrier, inc=1, device_id={"dp": place, "ctx": seat}, device_id_type=MESH)
    greeted = 2 * nb + len(line)

    pairs = (
        (pre_h, pre), (val_h, val), (post_h, post), (cot_h, cot), (filt_h, filt), (tw_h, tw),
        (e_h, e), (et_h, et), (ef_h, ef), (eft_h, eft), (t3_h, t3), (t3i_h, t3i),
    )
    loads = [pltpu.make_async_copy(s, d, in_sem.at[i]) for i, (s, d) in enumerate(pairs)]
    for load in loads:
        load.start()
    for load in loads[:5]:
        load.wait()
    xs[0] = (pre[...].astype(F32) * val[...].astype(F32)).astype(BF)
    xs[1] = (cot[...].astype(F32) * post[...].astype(F32)).astype(BF)
    lags = jnp.concatenate(
        [filt[:, i * TOKENS : (i + 1) * TOKENS] for i in range(own)], axis=0
    ).astype(BF)
    fbs[...] = lags
    mine = pl.multiple_of(dp * chunk, chunk)

    @pl.when(holder)
    def _():
        fb[pl.ds(mine, chunk), :] = lags

    pl.semaphore_wait(barrier, greeted)

    def wait_bytes(ref, sem):
        pltpu.make_async_copy(ref, ref, sem).wait()

    for k in range(groups // 2):
        place = core + 2 * k

        @pl.when(place != dp)
        def _():
            pltpu.make_async_remote_copy(
                src_ref=fbs,
                dst_ref=fb.at[pl.ds(mine, chunk), :],
                send_sem=send_sem.at[0],
                recv_sem=recv_sem.at[0],
                device_id={"dp": place, "ctx": ctx},
                device_id_type=MESH,
            ).start()

    landing = pl.ds(pl.multiple_of(ctx * ROWS + parity * 4, 4), 4)

    def row(m, part, signal, sem):
        return pltpu.make_async_remote_copy(
            src_ref=xs.at[signal, pl.ds(pl.multiple_of(m * ROWS + 4 * part, 4), 4), :],
            dst_ref=recv.at[landing, :],
            send_sem=sem,
            recv_sem=recv_sem.at[1],
            device_id={"dp": far + part, "ctx": 2 * m + signal},
            device_id_type=MESH,
        )

    def send_first(m, carry):
        for part in range(2):
            row(m, part, 0, row_sem.at[2 * m + part]).start()
        return carry

    def send_second(m, carry):
        for part in range(2):
            row(m, part, 0, row_sem.at[2 * m + part]).wait_send()
            row(m, part, 1, send_sem.at[1]).start()
        return carry

    lax.fori_loop(0, nb // 2, send_first, 0)

    for load in loads[5:]:
        load.wait()
    column = lax.broadcasted_iota(jnp.int32, (wide, nb * ROWS), 1)
    for s in range(ROWS):
        keep = ((column & (ROWS - 1)) == s).astype(F32)
        w[s * wide : (s + 1) * wide, :] = (e[...].astype(F32) * keep).astype(BF)
    column = lax.broadcasted_iota(jnp.int32, (wide, nb * 4), 1)
    for s in range(4):
        keep = ((column & 3) == s).astype(F32)
        wf[s * wide : (s + 1) * wide, :] = (ef[...].astype(F32) * keep).astype(BF)
    lax.fori_loop(0, nb // 2, send_second, 0)
    at = lax.broadcasted_iota(jnp.int32, (nb * ROWS, wide), 0)
    for s in range(ROWS):
        keep = ((at & (ROWS - 1)) == s).astype(F32)
        wt[:, s * wide : (s + 1) * wide] = (et[...].astype(F32) * keep).astype(BF)
    at = lax.broadcasted_iota(jnp.int32, (nb * 2, wide), 0)
    for s in range(2):
        keep = ((at & 1) == s).astype(F32)
        wtf[:, s * wide : (s + 1) * wide] = (eft[...].astype(F32) * keep).astype(BF)

    def forward(count, source, table, result):
        a[0 : count * wide, :] = dot(table[...], source[...])

        def one(s, carry):
            ar = a[pl.ds(pl.multiple_of(s * wide, wide), nb), :]
            ai = a[pl.ds(pl.multiple_of(s * wide + nb, nb), nb), :]
            tc, ts = tw[0], tw[1]
            rows = pl.ds(pl.multiple_of(s * nb, nb), nb)
            b[rows, 0:TOKENS] = (ar * tc + ai * ts).astype(BF)
            b[rows, TOKENS:] = (ai * tc - ar * ts).astype(BF)
            return carry

        lax.fori_loop(0, count, one, 0)
        result[...] = dot(b[0 : count * nb, :], t3[...])

    def backward(count):
        v = dot(prod[0 : count * nb, :], t3i[...])
        scale = 2.0 / (2 * nb * TOKENS)
        tc, ts = tw[0] * scale, tw[1] * scale
        for s in range(count):
            vr = v[s * nb : (s + 1) * nb, 0:TOKENS]
            vi = v[s * nb : (s + 1) * nb, TOKENS:]
            u[s * wide : s * wide + nb, :] = (vr * tc - vi * ts).astype(BF)
            u[s * wide + nb : (s + 1) * wide, :] = (vr * ts + vi * tc).astype(BF)

    swap = pltpu.make_async_remote_copy(
        src_ref=fb,
        dst_ref=fb,
        send_sem=send_sem.at[2],
        recv_sem=recv_sem.at[2],
        device_id={"dp": dp, "ctx": partner},
        device_id_type=MESH,
    )

    @pl.when(holder)
    def _():
        wait_bytes(fb.at[pl.ds(0, (groups - 1) * chunk), :], recv_sem.at[0])
        swap.start()

    @pl.when(jnp.logical_not(holder))
    def _():
        swap.wait_recv()

    forward(4, fb, wf, fspec)

    wait_bytes(recv, recv_sem.at[1])
    forward(ROWS, recv, w, spec)

    sign = (1 - 2 * core).astype(F32)
    two = 2 * nb
    four = 4 * nb
    theirs = pl.multiple_of((1 - core) * two, two)
    sx[0:two, :] = spec[pl.ds(theirs, two), :].astype(BF)
    sx[two:, :] = spec[pl.ds(four + theirs, two), :].astype(BF)
    fr, fi = fspec[:, 0:TOKENS], fspec[:, TOKENS:] * sign
    for j in range(2):
        rows = slice(j * four, (j + 1) * four)
        xr, xi = spec[rows, 0:TOKENS], spec[rows, TOKENS:]
        prod[rows, 0:TOKENS] = (fr * xr - fi * xi).astype(BF)
        prod[rows, TOKENS:] = (fr * xi + fi * xr).astype(BF)
    cross = pltpu.make_async_remote_copy(
        src_ref=sx,
        dst_ref=rx,
        send_sem=send_sem.at[3],
        recv_sem=recv_sem.at[3],
        device_id={"dp": dp, "ctx": partner},
        device_id_type=MESH,
    )
    cross.start()
    backward(ROWS)
    y[...] = dot(wt[...], u[...]).astype(BF)

    home = pl.ds(pl.multiple_of(chip * ROWS + parity * 4, 4), 4)

    def send_out(j, carry):
        for part in range(2):
            pltpu.make_async_remote_copy(
                src_ref=y.at[pl.ds(pl.multiple_of(j * ROWS + 4 * part, 4), 4), :],
                dst_ref=out_h.at[core, home, :],
                send_sem=send_sem.at[4],
                recv_sem=recv_sem.at[4],
                device_id={"dp": far + part, "ctx": j},
                device_id_type=MESH,
            ).start()
        return carry

    lax.fori_loop(0, nb, send_out, 0)

    cross.wait()
    ours = pl.multiple_of(core * two, two)
    real, imag = None, None
    for j in range(2):
        rows = pl.ds(four * j + ours, two)
        xr, xi = spec[rows, 0:TOKENS], spec[rows, TOKENS:]
        gr = rx[j * two : (j + 1) * two, 0:TOKENS].astype(F32)
        gi = rx[j * two : (j + 1) * two, TOKENS:].astype(F32)
        re, im = xr * gr + xi * gi, xr * gi - xi * gr
        real, imag = (re, im) if j == 0 else (real + re, imag + im)
    prod[0:two, 0:TOKENS] = real.astype(BF)
    prod[0:two, TOKENS:] = (imag * sign).astype(BF)
    backward(2)
    fgs[...] = dot(wtf[...], u[0 : 2 * wide, :]).astype(BF)
    slot = pl.ds(pl.multiple_of((2 * rank + core) * piece, piece), piece)
    self_piece = pltpu.make_async_copy(
        fgs.at[pl.ds(pl.multiple_of(dp * piece, piece), piece), :], fgr_h.at[slot, :], in_sem.at[2]
    )

    @pl.when(holder)
    def _():
        self_piece.start()

    for i in range(groups):
        peer = lax.rem(dp + i, groups)

        @pl.when((peer != dp) | jnp.logical_not(holder))
        def _():
            pltpu.make_async_remote_copy(
                src_ref=fgs.at[pl.ds(pl.multiple_of(peer * piece, piece), piece), :],
                dst_ref=fgr_h.at[slot, :],
                send_sem=send_sem.at[5],
                recv_sem=recv_sem.at[5],
                device_id={"dp": peer, "ctx": 2 * chip + parity},
                device_id_type=MESH,
            ).start()

    most = fgs.at[pl.ds(0, (groups - 1) * piece), :]

    @pl.when(holder)
    def _():
        self_piece.wait()
        swap.wait_send()
        wait_bytes(fb.at[pl.ds(0, (groups // 2 - 1) * chunk), :], send_sem.at[0])
        wait_bytes(most, send_sem.at[5])
        wait_bytes(most, recv_sem.at[5])

    @pl.when(jnp.logical_not(holder))
    def _():
        wait_bytes(fb.at[pl.ds(0, (groups // 2) * chunk), :], send_sem.at[0])
        wait_bytes(fgs, send_sem.at[5])
        wait_bytes(fgs, recv_sem.at[5])

    wait_bytes(xs.at[1], send_sem.at[1])
    wait_bytes(y, send_sem.at[4])
    wait_bytes(y, recv_sem.at[4])


def last_kernel(own, groups, pre, val, post, cot, back, fgr, mixed, pre_grad, value_grad, post_grad, filter_grad):
    conv = back[0].astype(F32)
    mixed[...] = (post[...].astype(F32) * conv).astype(BF)
    post_grad[...] = (cot[...].astype(F32) * conv).astype(BF)
    grad = back[1].astype(F32)
    pre_grad[...] = (grad * val[...].astype(F32)).astype(BF)
    value_grad[...] = (grad * pre[...].astype(F32)).astype(BF)
    rows = own * 4
    total = fgr[0:rows, :].astype(F32)
    for i in range(1, groups // 2):
        total = total + fgr[i * rows : (i + 1) * rows, :].astype(F32)
    for side in range(2):
        for i in range(own):
            at = (side * own + i) * 2
            filter_grad[2 * side : 2 * side + 2, i * TOKENS : (i + 1) * TOKENS] = total[at : at + 2, :]


def body(pre_gate, values, post_gate, filters, cotangent):
    nb = lax.axis_size("ctx")
    groups = lax.axis_size("dp")
    own = nb // groups
    rows = nb * 4
    consts = tables(nb, groups)
    anywhere = pl.BlockSpec(memory_space=pl.ANY)
    vmem = pl.BlockSpec(memory_space=pltpu.VMEM)
    sig = (rows, TOKENS)
    scratch = [
        pltpu.VMEM(sig, BF), pltpu.VMEM(sig, BF), pltpu.VMEM(sig, BF), pltpu.VMEM(sig, BF),
        pltpu.VMEM(filters.shape, F32),
        *[pltpu.VMEM(c.shape, BF) for c in consts[:6]],
        pltpu.VMEM(consts[6].shape, F32),
        pltpu.VMEM((2,) + sig, BF),
        pltpu.VMEM((nb * ROWS, TOKENS), BF),
        pltpu.VMEM((own * 4, TOKENS), BF),
        pltpu.VMEM((nb * 4, TOKENS), BF),
        pltpu.VMEM((ROWS * 2 * nb, nb * ROWS), BF),
        pltpu.VMEM((nb * ROWS, ROWS * 2 * nb), BF),
        pltpu.VMEM((4 * 2 * nb, nb * 4), BF),
        pltpu.VMEM((nb * 2, 2 * 2 * nb), BF),
        pltpu.VMEM((ROWS * 2 * nb, TOKENS), F32),
        pltpu.VMEM((ROWS * nb, 2 * TOKENS), BF),
        pltpu.VMEM((ROWS * nb, 2 * TOKENS), F32),
        pltpu.VMEM((4 * nb, 2 * TOKENS), F32),
        pltpu.VMEM((ROWS * nb, 2 * TOKENS), BF),
        pltpu.VMEM((ROWS * 2 * nb, TOKENS), BF),
        pltpu.VMEM((nb * ROWS, TOKENS), BF),
        pltpu.VMEM((4 * nb, 2 * TOKENS), BF),
        pltpu.VMEM((4 * nb, 2 * TOKENS), BF),
        pltpu.VMEM((nb * 2, TOKENS), BF),
        pltpu.SemaphoreType.DMA((12,)),
        pltpu.SemaphoreType.DMA((6,)),
        pltpu.SemaphoreType.DMA((6,)),
        pltpu.SemaphoreType.DMA((nb,)),
    ]
    back, fgr = pl.pallas_call(
        functools.partial(main_kernel, nb, groups),
        out_shape=(jax.ShapeDtypeStruct((2,) + sig, BF), jax.ShapeDtypeStruct((nb * 2, TOKENS), BF)),
        in_specs=[anywhere] * 12,
        out_specs=(anywhere, anywhere),
        scratch_shapes=scratch,
        compiler_params=pltpu.CompilerParams(collective_id=0, has_side_effects=True),
        name="long_conv",
    )(pre_gate, values, post_gate, cotangent, filters, *consts)
    shape = jax.ShapeDtypeStruct(pre_gate.shape, BF)
    mixed, pre_grad, value_grad, post_grad, filter_grad = pl.pallas_call(
        functools.partial(last_kernel, own, groups),
        out_shape=(shape, shape, shape, shape, jax.ShapeDtypeStruct(filters.shape, F32)),
        in_specs=[vmem] * 6,
        out_specs=(vmem,) * 5,
        name="gates",
    )(pre_gate, values, post_gate, cotangent, back, fgr)
    return (mixed, pre_grad, value_grad, post_grad, filter_grad)


def solution(mesh):
    big = P("dp", "ctx")
    return jax.shard_map(
        body,
        mesh=mesh,
        in_specs=(big, big, big, P("ctx", "dp"), big),
        out_specs=(big, big, big, big, P("ctx", "dp")),
        check_vma=False,
    )
```
